32 devices in a mesh: series: 4 (over y, x), tm: 8 (over z, core).
Axes of the slice: x: 2, y: 2, z: 4, core: 2. Of those that a mesh axis runs over, the one named last changes fastest.
Arguments:
- observed: bfloat16 [5120, 6144], P('series', 'tm'), may hold values from -6 to 6
- mask: int32 [5120, 6144], P('series', 'tm'), may hold values 0 or 1
- series_factors: float32 [5120, 256], P('series'), may hold values from -6 to 6
- time_factors: float32 [256, 6144], P(None, 'tm'), may hold values from -0.375 to 0.375
- ar_weights: float32 [3, 256], replicated, may hold values from -0.7 to 0.7
Outputs:
- series_out: float32 [5120, 256], P('series')
- time_out: float32 [256, 6144], P(None, 'tm')
- imputed: bfloat16 [5120, 6144], P('series', 'tm')
The draws below stay inside these ranges and needn't reach their ends.
Inputs may be any that keep to these rules, and one draw needn't show every extreme that they name: mask holds only 0 and 1.
All inputs are finite; a program needn't handle non-finite values. No bound on the sum of `mask` on one device may be relied on, other than what follows from the above.
Results may differ from the reference program's by a relative error of at most 0.0089.
Values sent between devices are 32-bit elements; how exact they have to be, the bound alone decides.
A program may use at most 128 MiB of HBM per device.

```python
import jax
import jax.numpy as jnp
from jax import lax

K = 256
ITERS = 2
SERIES = 5120
HOURS = 6144


def plant(values, stream_key, smallest, largest):
    spot = [jax.random.randint(jax.random.fold_in(stream_key, axis), (), 0, length) for axis, length in enumerate(values.shape)]
    longest = values.shape.index(max(values.shape))
    neighbour = spot[:longest] + [(spot[longest] + 1) % values.shape[longest]] + spot[longest + 1:]
    return values.at[tuple(spot)].set(smallest).at[tuple(neighbour)].set(largest)


def block_scale(stream_key, dims, cuts, least, top_value):
    def one(axis_at, blocks):
        heights = jax.random.uniform(jax.random.fold_in(jax.random.fold_in(stream_key, 6), axis_at), (blocks,), jnp.float32, least / len(cuts), top_value / len(cuts))
        return jnp.repeat(jnp.exp(heights), dims[axis_at] // blocks).reshape((-1,) + (1,) * (len(dims) - axis_at - 1))

    loudness = one(*cuts[0])
    for cut in cuts[1:]:
        loudness = loudness * one(*cut)
    return loudness


def noise(stream_key, dims, deviation, reach, split=(), dtype=jnp.bfloat16):
    values = jax.random.normal(stream_key, dims, jnp.float32) * deviation
    if len(split) > 0:
        values = block_scale(stream_key, dims, split, -0.22, 0.18) * values
    return jnp.clip(values, min=-reach, max=reach).astype(dtype)


def setup_inputs(seed: int = 0) -> dict:
    streams_of = jax.random.split(jax.random.key(seed), 6)
    return {
        "observed": noise(streams_of[0], (SERIES, HOURS), 1.0, 6.0, ((0, 4), (1, 8))),
        "mask": plant((jax.random.randint(streams_of[1], (SERIES, HOURS), 0, 2) < 1).astype(jnp.int32), jax.random.fold_in(streams_of[1], 1), 0, 1),
        "series_factors": noise(streams_of[2], (SERIES, K), 1.0, 6.0, ((0, 4),), jnp.float32),
        "time_factors": noise(streams_of[3], (K, HOURS), K ** -0.5, 0.375, ((1, 8),), jnp.float32),
        "ar_weights": jnp.clip(jax.random.uniform(streams_of[4], (3, K), jnp.float32, -0.7, 0.7), -0.7, 0.7),
    }


lag_hours = (1, 24, 168)


def lag_terms(factors, weights):
    hour_count = factors.shape[1]
    in_range = jnp.arange(hour_count) >= 168
    lag_resid = factors
    for lag_index, lag_size in enumerate(lag_hours):
        earlier = jnp.pad(factors, ((0, 0), (lag_size, 0)))[:, :hour_count]
        lag_resid = lag_resid - weights[lag_index][:, None] * earlier
    lag_resid = jnp.where(in_range[None, :], lag_resid, jnp.zeros_like(lag_resid))
    backward = jnp.zeros_like(lag_resid)
    for lag_index, lag_size in enumerate(lag_hours):
        later = jnp.pad(lag_resid, ((0, 0), (0, lag_size)))[:, lag_size:]
        backward = backward + weights[lag_index][:, None] * later
    return lag_resid, backward


def reference(observed, mask, series_factors, time_factors, ar_weights):
    sensor_count, hour_count = observed.shape
    factor_rank = time_factors.shape[0]
    step_f = factor_rank / hour_count
    step_x = 1.0 / sensor_count
    ridge_f = 0.1 * hour_count / factor_rank
    ridge_x = 0.1 * sensor_count
    lam_ar = sensor_count / 8.0
    series_now = series_factors
    time_now = time_factors
    for sweep in range(ITERS):
        series_low = series_now.astype(jnp.bfloat16)
        time_low = time_now.astype(jnp.bfloat16)
        product = jnp.dot(series_low, time_low, preferred_element_type=jnp.float32)
        misfit = jnp.where(mask != 0, product - observed.astype(jnp.float32), jnp.zeros_like(product)).astype(jnp.bfloat16)
        grad_series = lax.dot_general(misfit, time_low, (((1,), (1,)), ((), ())), preferred_element_type=jnp.float32)
        grad_data = lax.dot_general(series_low, misfit, (((0,), (0,)), ((), ())), preferred_element_type=jnp.float32)
        lag_resid, backward = lag_terms(time_now, ar_weights)
        series_next = series_now - step_f * (grad_series + ridge_f * series_now)
        time_next = time_now - step_x * (grad_data + ridge_x * time_now + lam_ar * (lag_resid - backward))
        series_now, time_now = series_next, time_next
    imputed = jnp.dot(series_now.astype(jnp.bfloat16), time_now.astype(jnp.bfloat16), preferred_element_type=jnp.float32).astype(jnp.bfloat16)
    return series_now, time_now, imputed
```

```python
import functools

import jax
import jax.numpy as jnp
from jax import lax
from jax.experimental import pallas as pl
from jax.experimental.pallas import tpu as pltpu
from jax.sharding import PartitionSpec as P

ITERS = 2
LAGS = (1, 24, 168)
HALO = 256
GROUP = 256
SUBS = 4
WIDTH = 256
LAG = 4
HOP = 3
TAIL_STEPS = 5
VMEM_BYTES = 67043328
VMEM_SPARE = 64 * 1024
Z_AT_G = ((1, 2, 3), (5, 6, 7))
Z_AT_AR = (5, 8)
Z_AT_X = (5, 8)
Z_PER_X = 2
Z_NEXT = (0, 0, 0, 2, 4)


def kernel(
    series_size, tm_size,
    obs_hbm, mask_hbm, f_hbm, x_hbm, w_in,
    f_out, x_out,
    obs, mask, f_in, x_in, f_mid, x_mid, ar, misfit, f_low, x_low, grad, partner_in, outer_in, inner_in,
    g_loc, up_in, cross_in, halo_l, halo_r, w_cols,
    load_sem, x_sem, pair_send, in_send, spread_send, give_send, up_send, cross_send, share_send, edge_send,
    pair_recv, give_recv, outer_recv, inner_recv, up_recv, cross_recv, share_recv, edge_recv,
):
    rows, rank = f_in.shape
    hours = x_in.shape[1]
    groups = rows // GROUP
    own = GROUP // 2
    sub = own // SUBS
    blocks = groups * SUBS
    parts = hours // WIDTH
    piece = rank // series_size
    hours_all = hours * tm_size
    sensors_all = rows * series_size
    step_f = rank / hours_all
    step_x = 1.0 / sensors_all
    ridge_f = 0.1 * hours_all / rank
    ridge_x = 0.1 * sensors_all
    lam_ar = sensors_all / 8.0

    s = lax.axis_index("series")
    tm = lax.axis_index("tm")
    core = tm % 2
    chip = tm // 2
    chips = tm_size // 2
    middle = chips // 2
    right = chip // middle
    toward = 1 - 2 * right
    distance = right * (chip - middle) + (1 - right) * (middle - 1 - chip)
    is_mid = distance == 0
    is_end = distance == middle - 1
    not_end = distance < middle - 1
    lag = LAG + HOP * distance
    last_lag = LAG + HOP * (middle - 1)
    partner = chip * 2 + (1 - core)
    inward = tm + 2 * toward
    outward = tm - 2 * toward

    half = series_size // 2
    high, low_bit = s // 2, s % 2
    place = (1 - low_bit) * high + low_bit * (series_size - 1 - high)

    def device_at(p):
        p = lax.rem(p + series_size, series_size)
        far = p // half
        return (1 - far) * 2 * p + far * (2 * (series_size - 1 - p) + 1)

    following, previous = device_at(place + 1), device_at(place - 1)

    def both(a, b):
        return jnp.logical_and(a, b)

    def remote(src, dst, ssem, rsem, series_to, tm_to):
        return pltpu.make_async_remote_copy(
            src_ref=src, dst_ref=dst, send_sem=ssem, recv_sem=rsem,
            device_id=(series_to, tm_to), device_id_type=pl.DeviceIdType.MESH,
        )

    def group_rows(g):
        return pl.ds(pl.multiple_of(g * GROUP, GROUP), GROUP)

    def own_rows(g, which):
        return pl.ds(pl.multiple_of(g * GROUP + which * own, own), own)

    def slot_group(g):
        return pl.ds(pl.multiple_of(g * own, own), own)

    def line_rows(j):
        return pl.ds(pl.multiple_of((j // SUBS) * GROUP + core * own + (j % SUBS) * sub, sub), sub)

    def slot_rows(j):
        return pl.ds(pl.multiple_of(j * sub, sub), sub)

    def piece_of(p):
        return lax.rem(place + series_size - p, series_size)

    def piece_rows(p):
        return pl.ds(pl.multiple_of(piece_of(p) * piece, piece), piece)

    def columns(c):
        return pl.ds(c * WIDTH, WIDTH)

    def load_copies(g):
        span = group_rows(g)
        return (
            pltpu.make_async_copy(f_hbm.at[span, :], f_in.at[span, :], load_sem.at[0, g]),
            pltpu.make_async_copy(mask_hbm.at[span, :], mask.at[span, :], load_sem.at[1, g]),
            pltpu.make_async_copy(obs_hbm.at[span, :], obs.at[span, :], load_sem.at[2, g]),
        )

    barrier = pltpu.get_barrier_semaphore()
    for d in (-2, -1, 1, 2):
        @pl.when(both(tm + d >= 0, tm + d < tm_size))
        def _():
            pl.semaphore_signal(barrier, inc=1, device_id=(s, tm + d), device_id_type=pl.DeviceIdType.MESH)
    for to in (following, previous):
        pl.semaphore_signal(barrier, inc=1, device_id=(to, tm), device_id_type=pl.DeviceIdType.MESH)

    x_load = pltpu.make_async_copy(x_hbm, x_in, x_sem.at[0])
    x_load.start()

    @pl.loop(0, groups)
    def _(g):
        for c in load_copies(g):
            c.start()

    x_load.wait()

    ar_rows = piece_rows(half - 1)

    def edge_copies(it, source):
        to_right = remote(
            source.at[ar_rows, pl.ds(hours - HALO, HALO)], halo_l.at[it],
            edge_send.at[it, 0], edge_recv.at[it, 0], s, tm + 1,
        )
        to_left = remote(
            source.at[ar_rows, pl.ds(0, HALO)], halo_r.at[it],
            edge_send.at[it, 1], edge_recv.at[it, 1], s, tm - 1,
        )
        return to_right, to_left

    def start_edges(it, source):
        to_right, to_left = edge_copies(it, source)
        pl.when(tm < tm_size - 1)(to_right.start)
        pl.when(tm > 0)(to_left.start)

    f_at = (f_in, f_mid, f_out)
    x_at = (x_in, x_mid, x_out)

    def pair_copy(it, g):
        return remote(
            grad.at[it, own_rows(g, 1 - core), :], partner_in.at[it, slot_group(g), :],
            pair_send.at[it], pair_recv.at[it, g], s, partner,
        )

    def send_inward(it, j):
        view = grad.at[it, line_rows(j), :]

        @pl.when(is_mid)
        def _():
            remote(view, inner_in.at[it, slot_rows(j), :], in_send.at[it], inner_recv.at[it, j], s, inward).start()

        @pl.when(jnp.logical_not(is_mid))
        def _():
            remote(view, outer_in.at[it, slot_rows(j), :], in_send.at[it], outer_recv.at[it, j], s, inward).start()

    def outward_copy(it, j):
        view = f_at[it + 1].at[line_rows(j), :]
        return remote(view, view, spread_send.at[it], inner_recv.at[it, j], s, outward)

    def give_copy(it, g, which):
        view = f_at[it + 1].at[own_rows(g, which), :]
        return remote(view, view, give_send.at[it], give_recv.at[it, g], s, partner)

    def merge(it, g):
        pair_copy(it, g).wait_recv()
        grad[it, own_rows(g, core), :] += partner_in[it, slot_group(g), :]

        @pl.when(is_end)
        def _():
            for k in range(SUBS):
                send_inward(it, g * SUBS + k)

    def line_step(it, j):
        @pl.when(both(not_end, j < blocks))
        def _():
            slot = outer_in.at[it, slot_rows(j), :]
            remote(slot, slot, in_send.at[it], outer_recv.at[it, j], s, inward).wait_recv()
            grad[it, line_rows(j), :] += outer_in[it, slot_rows(j), :]
            send_inward(it, j)

        i = j - lag

        @pl.when(both(i >= 0, i < blocks))
        def _():
            @pl.when(is_mid)
            def _():
                slot = inner_in.at[it, slot_rows(i), :]
                remote(slot, slot, in_send.at[it], inner_recv.at[it, i], s, inward).wait_recv()
                old = f_at[it][line_rows(i), :]
                total = grad[it, line_rows(i), :] + inner_in[it, slot_rows(i), :]
                f_at[it + 1][line_rows(i), :] = old - step_f * (total + ridge_f * old)

            @pl.when(jnp.logical_not(is_mid))
            def _():
                outward_copy(it, i).wait_recv()

            pl.when(not_end)(outward_copy(it, i).start)
            pl.when(i % SUBS == SUBS - 1)(give_copy(it, i // SUBS, core).start)

    line_done = [0] * ITERS

    def run_line(it, stop):
        stop = min(stop, blocks + last_lag)
        if stop > line_done[it]:
            def body(j, carry):
                line_step(it, j)
                return carry

            lax.fori_loop(line_done[it], stop, body, 0)
            line_done[it] = stop

    def row_pass(it, g):
        span = group_rows(g)
        low = f_at[it][span, :].astype(jnp.bfloat16)
        f_low[span, :] = low
        product = jnp.dot(low, x_low[...], preferred_element_type=jnp.float32)
        miss = jnp.where(
            mask[span, :] != 0,
            product - obs[span, :].astype(jnp.float32),
            jnp.zeros_like(product),
        ).astype(jnp.bfloat16)
        misfit[span, :] = miss
        grad[it, span, :] = lax.dot_general(
            miss, x_low[...], (((1,), (1,)), ((), ())), preferred_element_type=jnp.float32
        )

    def up_copy(it, p, c):
        forward = p < half
        to = p + 1 if forward else p - 1
        dst = up_in.at[it, to, :, columns(c)]
        return remote(
            g_loc.at[it, piece_rows(p), columns(c)], dst, up_send.at[it], up_recv.at[it, to, c],
            following if forward else previous, tm,
        )

    def cross_copy(it, p, c):
        forward = p < half
        side = 1 if forward else 0
        return remote(
            g_loc.at[it, piece_rows(p), columns(c)], cross_in.at[it, side, :, columns(c)],
            cross_send.at[it], cross_recv.at[it, side, c], following if forward else previous, tm,
        )

    def share_copy(it, p, c):
        forward = p < half
        to = p - 1 if forward else p + 1
        view = x_at[it + 1].at[piece_rows(p), columns(c)]
        return remote(
            view, view, share_send.at[it], share_recv.at[it, to, c], previous if forward else following, tm,
        )

    def up_wait(it, p, c):
        slot = up_in.at[it, p, :, columns(c)]
        remote(slot, slot, up_send.at[it], up_recv.at[it, p, c], following, tm).wait_recv()

    def cross_wait(it, side, c):
        slot = cross_in.at[it, side, :, columns(c)]
        remote(slot, slot, cross_send.at[it], cross_recv.at[it, side, c], following, tm).wait_recv()

    def share_wait(it, p, c):
        view = x_at[it + 1].at[piece_rows(p), columns(c)]
        remote(view, view, share_send.at[it], share_recv.at[it, p, c], following, tm).wait_recv()

    def collect(it, depth, c):
        for p in (depth, series_size - 1 - depth):
            up_wait(it, p, c)
            total = g_loc[it, piece_rows(p), columns(c)] + up_in[it, p, :, columns(c)]
            if p == half - 1:
                total = total + lam_ar * ar[:, columns(c)]
            g_loc[it, piece_rows(p), columns(c)] = total
            (cross_copy if depth == half - 1 else up_copy)(it, p, c).start()

    def update(it, c):
        for p in (half - 1, half):
            side = p // half
            cross_wait(it, side, c)
            total = g_loc[it, piece_rows(p), columns(c)] + cross_in[it, side, :, columns(c)]
            old = x_at[it][piece_rows(p), columns(c)]
            x_at[it + 1][piece_rows(p), columns(c)] = old - step_x * (total + ridge_x * old)
            share_copy(it, p, c).start()

    def share(it, depth, c):
        for p in (depth, series_size - 1 - depth):
            share_wait(it, p, c)
            if depth > 0:
                share_copy(it, p, c).start()

    def residuals(it):
        x_now = x_at[it]
        to_right, to_left = edge_copies(it, x_now)

        @pl.when(tm > 0)
        def _():
            to_right.wait_recv()

        @pl.when(tm == 0)
        def _():
            halo_l[it] = jnp.zeros_like(halo_l[it])

        @pl.when(tm < tm_size - 1)
        def _():
            to_left.wait_recv()

        @pl.when(tm == tm_size - 1)
        def _():
            halo_r[it] = jnp.zeros_like(halo_r[it])

        extended = jnp.concatenate([halo_l[it], x_now[ar_rows, :], halo_r[it]], axis=1)
        width = hours + 2 * HALO
        weights = [w_cols[lag_at, ar_rows, :][:, 0:1] for lag_at in range(3)]
        resid = extended
        for lag_at in range(3):
            resid = resid - weights[lag_at] * pltpu.roll(extended, LAGS[lag_at], 1)
        hour = lax.broadcasted_iota(jnp.int32, (piece, width), 1) + (tm * hours - HALO)
        resid = jnp.where(both(hour >= 168, hour < hours_all), resid, jnp.zeros_like(resid))
        back = None
        for lag_at in range(3):
            term = weights[lag_at] * pltpu.roll(resid, width - LAGS[lag_at], 1)
            back = term if back is None else back + term
        ar[...] = (resid - back)[:, HALO : HALO + hours]

    for it in range(ITERS):
        x_low[...] = x_at[it][...].astype(jnp.bfloat16)
        for g in range(groups):
            if it == 0:
                for c in load_copies(g):
                    c.wait()
            else:
                run_line(it - 1, (g + 1) * SUBS + last_lag)
                give_copy(it - 1, g, 1 - core).wait_recv()
            row_pass(it, g)
            if it == 0 and g == 0:
                neighbours = jnp.minimum(tm, 2) + jnp.minimum(tm_size - 1 - tm, 2)
                pl.semaphore_wait(barrier, 2 + neighbours)
                start_edges(0, x_in)
            pair_copy(it, g).start()
            if g > 0:
                merge(it, g - 1)
            if it > 0:
                run_line(it, Z_NEXT[min(g, len(Z_NEXT) - 1)])
        merge(it, groups - 1)
        for c in range(parts):
            g_loc[it, :, columns(c)] = lax.dot_general(
                f_low[...], misfit[:, columns(c)], (((0,), (0,)), ((), ())),
                preferred_element_type=jnp.float32,
            )
            for p in (0, series_size - 1):
                up_copy(it, p, c).start()
            run_line(it, Z_AT_G[it][min(c, 2)])
        if it == 0:
            for lag_at in range(3):
                w_cols[lag_at] = jnp.transpose(jnp.broadcast_to(w_in[lag_at : lag_at + 1, :], (128, rank)))
        residuals(it)
        run_line(it, Z_AT_AR[it])
        events = []
        for depth in range(1, half):
            events += [(collect, depth, c) for c in range(parts)]
        events += [(lambda it, _, c: update(it, c), 0, c) for c in range(parts)]
        for depth in range(half - 2, -1, -1):
            events += [(share, depth, c) for c in range(parts)]
        for e, (step, depth, c) in enumerate(events):
            run_line(it, Z_AT_X[it] + Z_PER_X * e)
            step(it, depth, c)
        if it < ITERS - 1:
            start_edges(it + 1, x_at[it + 1])
    run_line(ITERS - 1, blocks + last_lag)
    for g in range(groups):
        give_copy(ITERS - 1, g, 1 - core).wait_recv()

    for it in range(ITERS):
        to_right, to_left = edge_copies(it, x_at[it])
        pl.when(tm < tm_size - 1)(to_right.wait_send)
        pl.when(tm > 0)(to_left.wait_send)
        line = partner_in.at[it]
        for sem in (pair_send, in_send, give_send):
            remote(line, line, sem.at[it], pair_recv.at[it, 0], s, partner).wait_send()

        @pl.when(not_end)
        def _():
            remote(line, line, spread_send.at[it], pair_recv.at[it, 0], s, partner).wait_send()

        many = up_in.at[it, pl.ds(0, series_size - 2)]
        two = cross_in.at[it]
        for view, sem in ((many, up_send), (two, cross_send), (many, share_send)):
            remote(view, view, sem.at[it], cross_recv.at[it, 0, 0], following, tm).wait_send()


def final_product(f_ref, x_ref, f_out, x_out, imputed, x_low, low, copy_sem, out_sem):
    tall = f_ref.shape[0] // TAIL_STEPS
    copies = (
        pltpu.make_async_copy(f_ref, f_out, copy_sem.at[0]),
        pltpu.make_async_copy(x_ref, x_out, copy_sem.at[1]),
    )
    x_low[...] = x_ref[...].astype(jnp.bfloat16)
    outs = []
    for i in range(TAIL_STEPS):
        span = pl.ds(i * tall, tall)
        low[span, :] = jnp.dot(
            f_ref[span, :].astype(jnp.bfloat16), x_low[...], preferred_element_type=jnp.float32
        ).astype(jnp.bfloat16)
        outs.append(pltpu.make_async_copy(low.at[span, :], imputed.at[span, :], out_sem.at[i]))
        outs[-1].start()
        if i == 0:
            for c in copies:
                c.start()
    for c in (*copies, *outs):
        c.wait()


def solution(mesh):
    series_size, tm_size = mesh.shape["series"], mesh.shape["tm"]

    def local(observed, mask, series_factors, time_factors, ar_weights):
        rows, rank = series_factors.shape
        hours = time_factors.shape[1]
        groups = rows // GROUP
        blocks = groups * SUBS
        parts = hours // WIDTH
        piece = rank // series_size
        f32, bf16 = jnp.float32, jnp.bfloat16
        vmem = pl.BlockSpec(memory_space=pltpu.VMEM)
        hbm = pl.BlockSpec(memory_space=pltpu.HBM)
        dma = pltpu.SemaphoreType.DMA
        line = (ITERS, rows // 2, rank)
        f_last, x_last = pl.pallas_call(
            functools.partial(kernel, series_size, tm_size),
            out_shape=(pltpu.VMEM((rows, rank), f32), pltpu.VMEM((rank, hours), f32)),
            in_specs=[hbm, hbm, hbm, hbm, vmem],
            out_specs=(vmem, vmem),
            scratch_shapes=[
                pltpu.VMEM((rows, hours), bf16),
                pltpu.VMEM((rows, hours), jnp.int32),
                pltpu.VMEM((rows, rank), f32),
                pltpu.VMEM((rank, hours), f32),
                pltpu.VMEM((rows, rank), f32),
                pltpu.VMEM((rank, hours), f32),
                pltpu.VMEM((piece, hours), f32),
                pltpu.VMEM((rows, hours), bf16),
                pltpu.VMEM((rows, rank), bf16),
                pltpu.VMEM((rank, hours), bf16),
                pltpu.VMEM((ITERS, rows, rank), f32),
                pltpu.VMEM(line, f32),
                pltpu.VMEM(line, f32),
                pltpu.VMEM(line, f32),
                pltpu.VMEM((ITERS, rank, hours), f32),
                pltpu.VMEM((ITERS, series_size, piece, hours), f32),
                pltpu.VMEM((ITERS, 2, piece, hours), f32),
                pltpu.VMEM((ITERS, piece, HALO), f32),
                pltpu.VMEM((ITERS, piece, HALO), f32),
                pltpu.VMEM((3, rank, 128), f32),
                dma((3, groups)), dma((1,)),
                dma((ITERS,)), dma((ITERS,)), dma((ITERS,)), dma((ITERS,)),
                dma((ITERS,)), dma((ITERS,)), dma((ITERS,)), dma((ITERS, 2)),
                dma((ITERS, groups)), dma((ITERS, groups)),
                dma((ITERS, blocks)), dma((ITERS, blocks)),
                dma((ITERS, series_size, parts)), dma((ITERS, 2, parts)), dma((ITERS, series_size, parts)),
                dma((ITERS, 2)),
            ],
            compiler_params=pltpu.CompilerParams(
                collective_id=0, has_side_effects=True,
                vmem_limit_bytes=VMEM_BYTES - 4 * rank * (rows + hours) - VMEM_SPARE,
            ),
        )(observed, mask, series_factors, time_factors, ar_weights)
        anywhere = pl.BlockSpec(memory_space=pl.ANY)
        return tuple(pl.pallas_call(
            final_product,
            out_shape=(
                jax.ShapeDtypeStruct((rows, rank), f32),
                jax.ShapeDtypeStruct((rank, hours), f32),
                jax.ShapeDtypeStruct((rows, hours), bf16),
            ),
            in_specs=[vmem, vmem],
            out_specs=(anywhere, anywhere, anywhere),
            scratch_shapes=[
                pltpu.VMEM((rank, hours), bf16),
                pltpu.VMEM((rows, hours), bf16),
                dma((2,)),
                dma((TAIL_STEPS,)),
            ],
            compiler_params=pltpu.CompilerParams(vmem_limit_bytes=16 * 1024 * 1024),
        )(f_last, x_last))

    in_specs = (P("series", "tm"), P("series", "tm"), P("series", None), P(None, "tm"), P())
    out_specs = (P("series", None), P(None, "tm"), P("series", "tm"))
    return jax.shard_map(local, mesh=mesh, in_specs=in_specs, out_specs=out_specs, check_vma=False)
```

```python
import functools

import jax
import jax.numpy as jnp
from jax import lax
from jax.experimental import pallas as pl
from jax.experimental.pallas import tpu as pltpu
from jax.sharding import PartitionSpec as P

ITERS = 2
LAGS = (1, 24, 168)
HALO = 256
GROUP = 256
SUBS = 4
WIDTH = 256
LAG = 4
HOP = 5
TAIL_STEPS = 5
VMEM_BYTES = 67043328
VMEM_SPARE = 64 * 1024
Z_FIRST = 1
Z_AT_X = (1, 10)
Z_PER_X = 2
Z_MID = (18, 19, 20, 24)
Z_LAST = (6, 7)
VMEM_BYTES = 67043328
VMEM_SPARE = 64 * 1024


def kernel(
    series_size, tm_size,
    obs_hbm, mask_hbm, f_hbm, x_hbm, w_hbm,
    f_out, x_out,
    obs, mask, f_in, x_in, f_mid, x_mid, ar, misfit, f_low, x_low, grad, partner_in, outer_in, inner_in,
    g_loc, up_in, cross_in, halo_l, halo_r, w_in, w_cols,
    load_sem, pair_send, in_send, spread_send, give_send, up_send, cross_send, share_send, edge_send,
    pair_recv, give_recv, outer_recv, inner_recv, up_recv, cross_recv, share_recv, edge_recv,
):
    rows, rank = f_in.shape
    hours = x_in.shape[1]
    groups = rows // GROUP
    own = GROUP // 2
    sub = own // SUBS
    blocks = groups * SUBS
    parts = hours // WIDTH
    piece = rank // series_size
    hours_all = hours * tm_size
    sensors_all = rows * series_size
    step_f = rank / hours_all
    step_x = 1.0 / sensors_all
    ridge_f = 0.1 * hours_all / rank
    ridge_x = 0.1 * sensors_all
    lam_ar = sensors_all / 8.0

    s = lax.axis_index("series")
    tm = lax.axis_index("tm")
    core = tm % 2
    chip = tm // 2
    chips = tm_size // 2
    middle = chips // 2
    right = chip // middle
    toward = 1 - 2 * right
    distance = right * (chip - middle) + (1 - right) * (middle - 1 - chip)
    is_mid = distance == 0
    is_end = distance == middle - 1
    not_end = distance < middle - 1
    lag = LAG + HOP * distance
    last_lag = LAG + HOP * (middle - 1)
    partner = chip * 2 + (1 - core)
    inward = tm + 2 * toward
    outward = tm - 2 * toward

    half = series_size // 2
    high, low_bit = s // 2, s % 2
    place = (1 - low_bit) * high + low_bit * (series_size - 1 - high)

    def device_at(p):
        p = lax.rem(p + series_size, series_size)
        far = p // half
        return (1 - far) * 2 * p + far * (2 * (series_size - 1 - p) + 1)

    following, previous = device_at(place + 1), device_at(place - 1)

    def both(a, b):
        return jnp.logical_and(a, b)

    def remote(src, dst, ssem, rsem, series_to, tm_to):
        return pltpu.make_async_remote_copy(
            src_ref=src, dst_ref=dst, send_sem=ssem, recv_sem=rsem,
            device_id=(series_to, tm_to), device_id_type=pl.DeviceIdType.MESH,
        )

    def group_rows(g):
        return pl.ds(pl.multiple_of(g * GROUP, GROUP), GROUP)

    def own_rows(g, which):
        return pl.ds(pl.multiple_of(g * GROUP + which * own, own), own)

    def slot_group(g):
        return pl.ds(pl.multiple_of(g * own, own), own)

    def line_rows(j):
        return pl.ds(pl.multiple_of((j // SUBS) * GROUP + core * own + (j % SUBS) * sub, sub), sub)

    def slot_rows(j):
        return pl.ds(pl.multiple_of(j * sub, sub), sub)

    def piece_of(p):
        return lax.rem(place + series_size - p, series_size)

    def piece_rows(p):
        return pl.ds(pl.multiple_of(piece_of(p) * piece, piece), piece)

    def columns(c):
        return pl.ds(c * WIDTH, WIDTH)

    first_rows, other_rows = pl.ds(0, GROUP), pl.ds(GROUP, rows - GROUP)
    every_hour = pl.ds(0, hours)

    def load(k, hbm, vmem, row_span, hour_span):
        return pltpu.make_async_copy(hbm.at[row_span, hour_span], vmem.at[row_span, hour_span], load_sem.at[k])

    rank_span = pl.ds(0, rank)
    w_load = pltpu.make_async_copy(w_hbm, w_in, load_sem.at[1])
    x_load = pltpu.make_async_copy(x_hbm, x_in, load_sem.at[0])
    first_loads = (
        load(2, f_hbm, f_in, first_rows, rank_span),
        load(3, mask_hbm, mask, first_rows, every_hour),
        load(4, obs_hbm, obs, first_rows, every_hour),
    )
    f_load = load(5, f_hbm, f_in, other_rows, rank_span)

    def part_loads(c):
        return (
            load(6 + 2 * c, mask_hbm, mask, other_rows, columns(c)),
            load(7 + 2 * c, obs_hbm, obs, other_rows, columns(c)),
        )

    x_load.start()
    for load_copy in (*first_loads, f_load, *part_loads(0)):
        load_copy.start()

    barrier = pltpu.get_barrier_semaphore()
    for d in (-2, -1, 1, 2):
        @pl.when(both(tm + d >= 0, tm + d < tm_size))
        def _():
            pl.semaphore_signal(barrier, inc=1, device_id=(s, tm + d), device_id_type=pl.DeviceIdType.MESH)
    for to in (following, previous):
        pl.semaphore_signal(barrier, inc=1, device_id=(to, tm), device_id_type=pl.DeviceIdType.MESH)

    for c in range(1, parts):
        for load_copy in part_loads(c):
            load_copy.start()
    w_load.start()

    ar_rows = piece_rows(half - 1)

    def edge_copies(it, source):
        to_right = remote(
            source.at[ar_rows, pl.ds(hours - HALO, HALO)], halo_l.at[it],
            edge_send.at[it, 0], edge_recv.at[it, 0], s, tm + 1,
        )
        to_left = remote(
            source.at[ar_rows, pl.ds(0, HALO)], halo_r.at[it],
            edge_send.at[it, 1], edge_recv.at[it, 1], s, tm - 1,
        )
        return to_right, to_left

    def start_edges(it, source):
        to_right, to_left = edge_copies(it, source)
        pl.when(tm < tm_size - 1)(to_right.start)
        pl.when(tm > 0)(to_left.start)

    f_at = (f_in, f_mid, f_out)
    x_at = (x_in, x_mid, x_out)

    def pair_copy(it, g):
        return remote(
            grad.at[it, own_rows(g, 1 - core), :], partner_in.at[it, slot_group(g), :],
            pair_send.at[it], pair_recv.at[g], s, partner,
        )

    def inner_slot(it, j):
        return j + blocks * (1 - jnp.minimum(j // (LAG + 1), 1)) if it % 2 else j

    def send_inward(it, j):
        view = grad.at[it, line_rows(j), :]

        @pl.when(is_mid)
        def _():
            remote(view, inner_in.at[it, slot_rows(j), :], in_send.at[it], inner_recv.at[inner_slot(it, j)], s, inward).start()

        @pl.when(jnp.logical_not(is_mid))
        def _():
            remote(view, outer_in.at[it, slot_rows(j), :], in_send.at[it], outer_recv.at[j], s, inward).start()

    def outward_copy(it, j):
        view = f_at[it + 1].at[line_rows(j), :]
        return remote(view, view, spread_send.at[it], inner_recv.at[inner_slot(it, j)], s, outward)

    def give_copy(it, g, which):
        view = f_at[it + 1].at[own_rows(g, which), :]
        return remote(view, view, give_send.at[it], give_recv.at[g], s, partner)

    def merge(it, g):
        pair_copy(it, g).wait_recv()
        grad[it, own_rows(g, core), :] += partner_in[it, slot_group(g), :]

        @pl.when(is_end)
        def _():
            for k in range(SUBS):
                send_inward(it, g * SUBS + k)

    def line_step(it, j):
        @pl.when(both(not_end, j < blocks))
        def _():
            slot = outer_in.at[it, slot_rows(j), :]
            remote(slot, slot, in_send.at[it], outer_recv.at[j], s, inward).wait_recv()
            grad[it, line_rows(j), :] += outer_in[it, slot_rows(j), :]
            send_inward(it, j)

        i = j - lag

        @pl.when(both(i >= 0, i < blocks))
        def _():
            @pl.when(is_mid)
            def _():
                slot = inner_in.at[it, slot_rows(i), :]
                remote(slot, slot, in_send.at[it], inner_recv.at[inner_slot(it, i)], s, inward).wait_recv()
                old = f_at[it][line_rows(i), :]
                total = grad[it, line_rows(i), :] + inner_in[it, slot_rows(i), :]
                f_at[it + 1][line_rows(i), :] = old - step_f * (total + ridge_f * old)

            @pl.when(jnp.logical_not(is_mid))
            def _():
                outward_copy(it, i).wait_recv()

            pl.when(not_end)(outward_copy(it, i).start)
            pl.when(i % SUBS == SUBS - 1)(give_copy(it, i // SUBS, core).start)

    line_done = [0] * ITERS

    def run_both(stop):
        stop = min(stop, blocks + last_lag)
        start = line_done[0]
        if stop > start:
            def body(j, carry):
                line_step(0, start + j)
                line_step(1, j)
                return carry

            lax.fori_loop(0, stop - start, body, 0)
            line_done[0], line_done[1] = stop, stop - start

    def run_line(it, stop):
        stop = min(stop, blocks + last_lag)
        if stop > line_done[it]:
            def body(j, carry):
                line_step(it, j)
                return carry

            lax.fori_loop(line_done[it], stop, body, 0)
            line_done[it] = stop

    def products(it, which):
        for g in which:
            span = group_rows(g)
            low = f_at[it][span, :].astype(jnp.bfloat16)
            f_low[span, :] = low
            product = jnp.dot(low, x_low[...], preferred_element_type=jnp.float32)
            misfit[span, :] = jnp.where(
                mask[span, :] != 0,
                product - obs[span, :].astype(jnp.float32),
                jnp.zeros_like(product),
            ).astype(jnp.bfloat16)

    def products_part(which, c):
        for g in which:
            span = group_rows(g)
            if c == 0:
                f_low[span, :] = f_in[span, :].astype(jnp.bfloat16)
            product = jnp.dot(f_low[span, :], x_low[:, columns(c)], preferred_element_type=jnp.float32)
            misfit[span, columns(c)] = jnp.where(
                mask[span, columns(c)] != 0,
                product - obs[span, columns(c)].astype(jnp.float32),
                jnp.zeros_like(product),
            ).astype(jnp.bfloat16)

    def series_grads(it, which):
        for g in which:
            span = group_rows(g)
            grad[it, span, :] = lax.dot_general(
                misfit[span, :], x_low[...], (((1,), (1,)), ((), ())), preferred_element_type=jnp.float32
            )

    def hour_grads(it, which):
        for g in which:
            span = group_rows(g)
            term = lax.dot_general(
                f_low[span, :], misfit[span, :], (((0,), (0,)), ((), ())), preferred_element_type=jnp.float32
            )
            if g > 0:
                term = g_loc[it] + term
            g_loc[it] = term

    def hour_grads_part(it, c):
        g_loc[it, :, columns(c)] = lax.dot_general(
            f_low[...], misfit[:, columns(c)], (((0,), (0,)), ((), ())), preferred_element_type=jnp.float32
        )

    def start_pairs(it, which):
        for g in which:
            pair_copy(it, g).start()

    def start_up(it, c):
        for p in (0, series_size - 1):
            up_copy(it, p, c).start()

    def up_copy(it, p, c):
        forward = p < half
        to = p + 1 if forward else p - 1
        dst = up_in.at[it, to, :, columns(c)]
        return remote(
            g_loc.at[it, piece_rows(p), columns(c)], dst, up_send.at[it], up_recv.at[to - 1, c],
            following if forward else previous, tm,
        )

    def cross_copy(it, p, c):
        forward = p < half
        side = 1 if forward else 0
        return remote(
            g_loc.at[it, piece_rows(p), columns(c)], cross_in.at[it, side, :, columns(c)],
            cross_send.at[it], cross_recv.at[side, c], following if forward else previous, tm,
        )

    def share_slot(p):
        return p if p < half else p - 2

    def share_copy(it, p, c):
        forward = p < half
        to = p - 1 if forward else p + 1
        view = x_at[it + 1].at[piece_rows(p), columns(c)]
        return remote(
            view, view, share_send.at[it], share_recv.at[share_slot(to), c], previous if forward else following, tm,
        )

    def up_wait(it, p, c):
        slot = up_in.at[it, p, :, columns(c)]
        remote(slot, slot, up_send.at[it], up_recv.at[p - 1, c], following, tm).wait_recv()

    def cross_wait(it, side, c):
        slot = cross_in.at[it, side, :, columns(c)]
        remote(slot, slot, cross_send.at[it], cross_recv.at[side, c], following, tm).wait_recv()

    def share_wait(it, p, c):
        view = x_at[it + 1].at[piece_rows(p), columns(c)]
        remote(view, view, share_send.at[it], share_recv.at[share_slot(p), c], following, tm).wait_recv()

    def collect(it, depth, c):
        for p in (depth, series_size - 1 - depth):
            up_wait(it, p, c)
            total = g_loc[it, piece_rows(p), columns(c)] + up_in[it, p, :, columns(c)]
            if p == half - 1:
                total = total + lam_ar * ar[:, columns(c)]
            g_loc[it, piece_rows(p), columns(c)] = total
            (cross_copy if depth == half - 1 else up_copy)(it, p, c).start()

    def update(it, c):
        for p in (half - 1, half):
            side = p // half
            cross_wait(it, side, c)
            total = g_loc[it, piece_rows(p), columns(c)] + cross_in[it, side, :, columns(c)]
            old = x_at[it][piece_rows(p), columns(c)]
            x_at[it + 1][piece_rows(p), columns(c)] = old - step_x * (total + ridge_x * old)
            share_copy(it, p, c).start()

    def share(it, depth, c):
        for p in (depth, series_size - 1 - depth):
            share_wait(it, p, c)
            if depth > 0:
                share_copy(it, p, c).start()

    def residuals(it):
        x_now = x_at[it]
        to_right, to_left = edge_copies(it, x_now)

        @pl.when(tm > 0)
        def _():
            to_right.wait_recv()

        @pl.when(tm == 0)
        def _():
            halo_l[it] = jnp.zeros_like(halo_l[it])

        @pl.when(tm < tm_size - 1)
        def _():
            to_left.wait_recv()

        @pl.when(tm == tm_size - 1)
        def _():
            halo_r[it] = jnp.zeros_like(halo_r[it])

        extended = jnp.concatenate([halo_l[it], x_now[ar_rows, :], halo_r[it]], axis=1)
        width = hours + 2 * HALO
        weights = [w_cols[lag_at, ar_rows, :][:, 0:1] for lag_at in range(3)]
        resid = extended
        for lag_at in range(3):
            resid = resid - weights[lag_at] * pltpu.roll(extended, LAGS[lag_at], 1)
        hour = lax.broadcasted_iota(jnp.int32, (piece, width), 1) + (tm * hours - HALO)
        resid = jnp.where(both(hour >= 168, hour < hours_all), resid, jnp.zeros_like(resid))
        back = None
        for lag_at in range(3):
            term = weights[lag_at] * pltpu.roll(resid, width - LAGS[lag_at], 1)
            back = term if back is None else back + term
        ar[...] = (resid - back)[:, HALO : HALO + hours]

    ns = jax.named_scope

    def x_events(it):
        events = []
        for depth in range(1, half):
            events += [(collect, depth, c) for c in range(parts)]
        events += [(lambda it, _, c: update(it, c), 0, c) for c in range(parts)]
        for depth in range(half - 2, -1, -1):
            events += [(share, depth, c) for c in range(parts)]
        for e, (step, depth, c) in enumerate(events):
            with ns(f"zx{it}_{e}"):
                run_line(it, Z_AT_X[it] + Z_PER_X * e)
            with ns(f"x{it}_{e}"):
                step(it, depth, c)

    every = tuple(range(groups))
    body_groups, next_last, last = every[1:-2], every[-2], every[-1]

    with ns("xload"):
        x_load.wait()
    x_low[...] = x_in[...].astype(jnp.bfloat16)
    with ns("load0"):
        for load_copy in first_loads:
            load_copy.wait()
    with ns("p0_0"):
        products(0, every[:1])
        series_grads(0, every[:1])
    with ns("barrier"):
        neighbours = jnp.minimum(tm, 2) + jnp.minimum(tm_size - 1 - tm, 2)
        pl.semaphore_wait(barrier, 2 + neighbours)
    start_pairs(0, every[:1])
    start_edges(0, x_in)
    with ns("load1"):
        f_load.wait()
    for c in range(parts):
        with ns(f"load2_{c}"):
            for load_copy in part_loads(c):
                load_copy.wait()
        with ns(f"p0_{c + 1}"):
            products_part(every[1:], c)
        if c == parts - 1:
            with ns("f0_1"):
                series_grads(0, every[1:2])
            start_pairs(0, every[1:2])
        with ns(f"g0_{c}"):
            hour_grads_part(0, c)
        start_up(0, c)
        if c == 0:
            with ns("m0_0"):
                merge(0, 0)
    with ns("f0_r"):
        series_grads(0, every[2:])
    start_pairs(0, every[2:])
    with ns("m0_1"):
        merge(0, 1)
    with ns("ar0"):
        w_load.wait()
        for lag_at in range(3):
            w_cols[lag_at] = jnp.transpose(jnp.broadcast_to(w_in[lag_at : lag_at + 1, :], (128, rank)))
        residuals(0)
    with ns("z0_a"):
        run_line(0, Z_FIRST)
    with ns("m0_r"):
        for g in every[2:]:
            merge(0, g)
    x_events(0)
    start_edges(1, x_mid)

    x_low[...] = x_mid[...].astype(jnp.bfloat16)
    def take(g):
        run_line(0, (g + 1) * SUBS + last_lag)
        give_copy(0, g, 1 - core).wait_recv()

    for g in every[:-2]:
        with ns(f"t1_{g}"):
            take(g)
        with ns(f"p1_{g}"):
            products(1, (g,))
            series_grads(1, (g,))
        start_pairs(1, (g,))
        with ns(f"zm1_{g}"):
            run_line(0, Z_MID[min(g, len(Z_MID) - 1)])
        if g > 0:
            with ns(f"m1_{g - 1}"):
                merge(1, g - 1)
    with ns("g1_a"):
        hour_grads(1, every[:-2])
    with ns("t1_c"):
        run_line(0, Z_MID[-1])
        take(next_last)
    with ns("ar1"):
        residuals(1)
    with ns("p1_c"):
        products(1, (next_last,))
        series_grads(1, (next_last,))
    start_pairs(1, (next_last,))
    with ns("m1_b"):
        merge(1, next_last - 1)
    with ns("t1_d"):
        run_both((last + 1) * SUBS + last_lag)
        take(last)
    with ns("p1_d"):
        products(1, (last,))
        hour_grads(1, (next_last, last))
    for c in range(parts):
        start_up(1, c)
    with ns("z1_a"):
        run_line(1, Z_LAST[0])
    with ns("f1_d"):
        series_grads(1, (last,))
    start_pairs(1, (last,))
    with ns("m1_c"):
        merge(1, next_last)
    with ns("z1_b"):
        run_line(1, Z_LAST[1])
    with ns("m1_d"):
        merge(1, last)
    x_events(1)
    with ns("zend"):
        run_line(1, blocks + last_lag)
    with ns("gend"):
        for g in every:
            give_copy(1, g, 1 - core).wait_recv()
    sc = ns("drain"); sc.__enter__()

    for it in range(ITERS):
        to_right, to_left = edge_copies(it, x_at[it])
        pl.when(tm < tm_size - 1)(to_right.wait_send)
        pl.when(tm > 0)(to_left.wait_send)
        line = partner_in.at[it]
        for sem in (pair_send, in_send, give_send):
            remote(line, line, sem.at[it], pair_recv.at[0], s, partner).wait_send()

        @pl.when(not_end)
        def _():
            remote(line, line, spread_send.at[it], pair_recv.at[0], s, partner).wait_send()

        many = up_in.at[it, pl.ds(0, series_size - 2)]
        two = cross_in.at[it]
        for view, sem in ((many, up_send), (two, cross_send), (many, share_send)):
            remote(view, view, sem.at[it], cross_recv.at[0, 0], following, tm).wait_send()
    sc.__exit__(None, None, None)


def final_product(f_ref, x_ref, f_out, x_out, imputed, x_low, low, copy_sem, out_sem):
    tall = f_ref.shape[0] // TAIL_STEPS
    copies = (
        pltpu.make_async_copy(f_ref, f_out, copy_sem.at[0]),
        pltpu.make_async_copy(x_ref, x_out, copy_sem.at[1]),
    )
    x_low[...] = x_ref[...].astype(jnp.bfloat16)
    outs = []
    for i in range(TAIL_STEPS):
        span = pl.ds(i * tall, tall)
        low[span, :] = jnp.dot(
            f_ref[span, :].astype(jnp.bfloat16), x_low[...], preferred_element_type=jnp.float32
        ).astype(jnp.bfloat16)
        outs.append(pltpu.make_async_copy(low.at[span, :], imputed.at[span, :], out_sem.at[i]))
        outs[-1].start()
        if i == 0:
            for c in copies:
                c.start()
    for c in (*copies, *outs):
        c.wait()


def solution(mesh):
    series_size, tm_size = mesh.shape["series"], mesh.shape["tm"]

    def local(observed, mask, series_factors, time_factors, ar_weights):
        rows, rank = series_factors.shape
        hours = time_factors.shape[1]
        groups = rows // GROUP
        blocks = groups * SUBS
        parts = hours // WIDTH
        piece = rank // series_size
        f32, bf16 = jnp.float32, jnp.bfloat16
        vmem = pl.BlockSpec(memory_space=pltpu.VMEM)
        hbm = pl.BlockSpec(memory_space=pltpu.HBM)
        dma = pltpu.SemaphoreType.DMA
        line = (ITERS, rows // 2, rank)
        f_last, x_last = pl.pallas_call(
            functools.partial(kernel, series_size, tm_size),
            out_shape=(pltpu.VMEM((rows, rank), f32), pltpu.VMEM((rank, hours), f32)),
            in_specs=[hbm] * 5,
            out_specs=(vmem, vmem),
            scratch_shapes=[
                pltpu.VMEM((rows, hours), bf16),
                pltpu.VMEM((rows, hours), jnp.int32),
                pltpu.VMEM((rows, rank), f32),
                pltpu.VMEM((rank, hours), f32),
                pltpu.VMEM((rows, rank), f32),
                pltpu.VMEM((rank, hours), f32),
                pltpu.VMEM((piece, hours), f32),
                pltpu.VMEM((rows, hours), bf16),
                pltpu.VMEM((rows, rank), bf16),
                pltpu.VMEM((rank, hours), bf16),
                pltpu.VMEM((ITERS, rows, rank), f32),
                pltpu.VMEM(line, f32),
                pltpu.VMEM(line, f32),
                pltpu.VMEM(line, f32),
                pltpu.VMEM((ITERS, rank, hours), f32),
                pltpu.VMEM((ITERS, series_size, piece, hours), f32),
                pltpu.VMEM((ITERS, 2, piece, hours), f32),
                pltpu.VMEM((ITERS, piece, HALO), f32),
                pltpu.VMEM((ITERS, piece, HALO), f32),
                pltpu.VMEM((3, rank), f32),
                pltpu.VMEM((3, rank, 128), f32),
                dma((6 + 2 * parts,)),
                dma((ITERS,)), dma((ITERS,)), dma((ITERS,)), dma((ITERS,)),
                dma((ITERS,)), dma((ITERS,)), dma((ITERS,)), dma((ITERS, 2)),
                dma((groups,)), dma((groups,)),
                dma((blocks,)), dma((blocks + LAG + 1,)),
                dma((series_size - 2, parts)), dma((2, parts)), dma((series_size - 2, parts)),
                dma((ITERS, 2)),
            ],
            compiler_params=pltpu.CompilerParams(
                collective_id=0, has_side_effects=True,
                vmem_limit_bytes=VMEM_BYTES - 4 * rank * (rows + hours) - VMEM_SPARE,
            ),
        )(observed, mask, series_factors, time_factors, ar_weights)
        anywhere = pl.BlockSpec(memory_space=pl.ANY)
        return tuple(pl.pallas_call(
            final_product,
            out_shape=(
                jax.ShapeDtypeStruct((rows, rank), f32),
                jax.ShapeDtypeStruct((rank, hours), f32),
                jax.ShapeDtypeStruct((rows, hours), bf16),
            ),
            in_specs=[vmem, vmem],
            out_specs=(anywhere, anywhere, anywhere),
            scratch_shapes=[
                pltpu.VMEM((rank, hours), bf16),
                pltpu.VMEM((rows, hours), bf16),
                dma((2,)),
                dma((TAIL_STEPS,)),
            ],
            compiler_params=pltpu.CompilerParams(vmem_limit_bytes=16 * 1024 * 1024),
        )(f_last, x_last))

    in_specs = (P("series", "tm"), P("series", "tm"), P("series", None), P(None, "tm"), P())
    out_specs = (P("series", None), P(None, "tm"), P("series", "tm"))
    return jax.shard_map(local, mesh=mesh, in_specs=in_specs, out_specs=out_specs, check_vma=False)
```

```python
import functools

import jax
import jax.numpy as jnp
from jax import lax
from jax.experimental import pallas as pl
from jax.experimental.pallas import tpu as pltpu
from jax.sharding import PartitionSpec as P

ITERS = 2
LAGS = (1, 24, 168)
HALO = 256
GROUP = 256
SUBS = 4
WIDTH = 256
LAG = 4
HOP = 5
TALL = 512
VMEM_BYTES = 67043328
VMEM_SPARE = 64 * 1024
Z_FIRST = 1
Z_AT_X = (1, 14)
Z_PER_X = 2
Z_MID = (18, 19, 20, 24)
Z_NEXT = 1
Z_LAST = (6, 7, 8)
VMEM_BYTES = 67043328
VMEM_SPARE = 64 * 1024


def kernel(
    series_size, tm_size,
    obs_hbm, mask_hbm, f_hbm, x_hbm, w_hbm,
    f_out, x_out,
    obs, mask, f_in, x_in, f_mid, x_mid, ar, misfit, f_low, x_low, grad, partner_in, outer_in, inner_in,
    g_loc, up_in, cross_in, halo_l, halo_r, w_in, w_cols,
    load_sem,
    pair_recv, give_recv, outer_recv, inner_recv, up_recv, cross_recv, share_recv, edge_recv,
):
    rows, rank = f_in.shape
    hours = x_in.shape[1]
    groups = rows // GROUP
    own = GROUP // 2
    sub = own // SUBS
    blocks = groups * SUBS
    parts = hours // WIDTH
    piece = rank // series_size
    hours_all = hours * tm_size
    sensors_all = rows * series_size
    step_f = rank / hours_all
    step_x = 1.0 / sensors_all
    ridge_f = 0.1 * hours_all / rank
    ridge_x = 0.1 * sensors_all
    lam_ar = sensors_all / 8.0

    pair_send, right_send, left_send, in_send, up_send, give_send, spread_send, cross_send, share_send = (
        load_sem.at[k] for k in (0, 2, 3, 4, 5, 6, 7, 8, 9)
    )
    s = lax.axis_index("series")
    tm = lax.axis_index("tm")
    core = tm % 2
    chip = tm // 2
    chips = tm_size // 2
    middle = chips // 2
    right = chip // middle
    toward = 1 - 2 * right
    distance = right * (chip - middle) + (1 - right) * (middle - 1 - chip)
    is_mid = distance == 0
    is_end = distance == middle - 1
    not_end = distance < middle - 1
    lag = LAG + HOP * distance
    last_lag = LAG + HOP * (middle - 1)
    partner = chip * 2 + (1 - core)
    inward = tm + 2 * toward
    outward = tm - 2 * toward

    half = series_size // 2
    high, low_bit = s // 2, s % 2
    place = (1 - low_bit) * high + low_bit * (series_size - 1 - high)

    def device_at(p):
        p = lax.rem(p + series_size, series_size)
        far = p // half
        return (1 - far) * 2 * p + far * (2 * (series_size - 1 - p) + 1)

    following, previous = device_at(place + 1), device_at(place - 1)

    def both(a, b):
        return jnp.logical_and(a, b)

    def remote(src, dst, ssem, rsem, series_to, tm_to):
        return pltpu.make_async_remote_copy(
            src_ref=src, dst_ref=dst, send_sem=ssem, recv_sem=rsem,
            device_id=(series_to, tm_to), device_id_type=pl.DeviceIdType.MESH,
        )

    def group_rows(g):
        return pl.ds(pl.multiple_of(g * GROUP, GROUP), GROUP)

    def own_rows(g, which):
        return pl.ds(pl.multiple_of(g * GROUP + which * own, own), own)

    def slot_group(g):
        return pl.ds(pl.multiple_of(g * own, own), own)

    def line_rows(j):
        return pl.ds(pl.multiple_of((j // SUBS) * GROUP + core * own + (j % SUBS) * sub, sub), sub)

    def slot_rows(j):
        return pl.ds(pl.multiple_of(j * sub, sub), sub)

    def piece_of(p):
        return lax.rem(place + series_size - p, series_size)

    def piece_rows(p):
        return pl.ds(pl.multiple_of(piece_of(p) * piece, piece), piece)

    def columns(c):
        return pl.ds(c * WIDTH, WIDTH)

    first_rows, other_rows = pl.ds(0, GROUP), pl.ds(GROUP, rows - GROUP)
    every_hour = pl.ds(0, hours)

    def load(k, hbm, vmem, row_span, hour_span):
        return pltpu.make_async_copy(hbm.at[row_span, hour_span], vmem.at[row_span, hour_span], load_sem.at[k])

    rank_span = pl.ds(0, rank)
    w_load = pltpu.make_async_copy(w_hbm, w_in, load_sem.at[1])
    x_load = pltpu.make_async_copy(x_hbm, x_in, load_sem.at[0])
    first_loads = (
        load(2, f_hbm, f_in, first_rows, rank_span),
        load(3, mask_hbm, mask, first_rows, every_hour),
        load(4, obs_hbm, obs, first_rows, every_hour),
    )
    f_load = load(5, f_hbm, f_in, other_rows, rank_span)

    def part_loads(c):
        return (
            load(6 + 2 * c, mask_hbm, mask, other_rows, columns(c)),
            load(7 + 2 * c, obs_hbm, obs, other_rows, columns(c)),
        )

    x_load.start()
    for load_copy in (*first_loads, f_load, *part_loads(0)):
        load_copy.start()

    barrier = pltpu.get_barrier_semaphore()
    for d in (-2, -1, 1, 2):
        @pl.when(both(tm + d >= 0, tm + d < tm_size))
        def _():
            pl.semaphore_signal(barrier, inc=1, device_id=(s, tm + d), device_id_type=pl.DeviceIdType.MESH)
    for to in (following, previous):
        pl.semaphore_signal(barrier, inc=1, device_id=(to, tm), device_id_type=pl.DeviceIdType.MESH)

    for c in range(1, parts):
        for load_copy in part_loads(c):
            load_copy.start()
    w_load.start()

    ar_rows = piece_rows(half - 1)

    def edge_copies(it, source):
        to_right = remote(
            source.at[ar_rows, pl.ds(hours - HALO, HALO)], halo_l.at[it],
            right_send, edge_recv.at[it, 0], s, tm + 1,
        )
        to_left = remote(
            source.at[ar_rows, pl.ds(0, HALO)], halo_r.at[it],
            left_send, edge_recv.at[it, 1], s, tm - 1,
        )
        return to_right, to_left

    right_out = both(right == 1, core == 1)
    left_out = both(right == 0, core == 0)

    def start_edges(it, source):
        to_right, to_left = edge_copies(it, source)
        pl.when(both(tm < tm_size - 1, jnp.logical_not(right_out)))(to_right.start)
        pl.when(both(tm > 0, jnp.logical_not(left_out)))(to_left.start)

    def start_outward_edges(it, source):
        to_right, to_left = edge_copies(it, source)
        pl.when(both(tm < tm_size - 1, right_out))(to_right.start)
        pl.when(both(tm > 0, left_out))(to_left.start)

    f_at = (f_in, f_mid, f_out)
    x_at = (x_in, x_mid, x_out)

    def pair_copy(it, g):
        return remote(
            grad.at[it, own_rows(g, 1 - core), :], partner_in.at[it, slot_group(g), :],
            pair_send, pair_recv.at[g], s, partner,
        )

    def inner_slot(it, j):
        return j + blocks * (1 - jnp.minimum(j // (LAG + 1), 1)) if it % 2 else j

    def send_inward(it, j):
        view = grad.at[it, line_rows(j), :]

        @pl.when(is_mid)
        def _():
            remote(view, inner_in.at[it, slot_rows(j), :], in_send, inner_recv.at[inner_slot(it, j)], s, inward).start()

        @pl.when(jnp.logical_not(is_mid))
        def _():
            remote(view, outer_in.at[it, slot_rows(j), :], in_send, outer_recv.at[j], s, inward).start()

    def outward_copy(it, j):
        view = f_at[it + 1].at[line_rows(j), :]
        return remote(view, view, spread_send, inner_recv.at[inner_slot(it, j)], s, outward)

    def give_copy(it, g, which):
        view = f_at[it + 1].at[own_rows(g, which), :]
        return remote(view, view, give_send, give_recv.at[g], s, partner)

    def merge(it, g):
        pair_copy(it, g).wait_recv()
        grad[it, own_rows(g, core), :] += partner_in[it, slot_group(g), :]

        @pl.when(is_end)
        def _():
            for k in range(SUBS):
                send_inward(it, g * SUBS + k)

    def line_step(it, j):
        @pl.when(both(not_end, j < blocks))
        def _():
            slot = outer_in.at[it, slot_rows(j), :]
            remote(slot, slot, in_send, outer_recv.at[j], s, inward).wait_recv()
            grad[it, line_rows(j), :] += outer_in[it, slot_rows(j), :]
            send_inward(it, j)

        i = j - lag

        @pl.when(both(i >= 0, i < blocks))
        def _():
            @pl.when(is_mid)
            def _():
                slot = inner_in.at[it, slot_rows(i), :]
                remote(slot, slot, in_send, inner_recv.at[inner_slot(it, i)], s, inward).wait_recv()
                old = f_at[it][line_rows(i), :]
                total = grad[it, line_rows(i), :] + inner_in[it, slot_rows(i), :]
                f_at[it + 1][line_rows(i), :] = old - step_f * (total + ridge_f * old)

            @pl.when(jnp.logical_not(is_mid))
            def _():
                outward_copy(it, i).wait_recv()

            pl.when(not_end)(outward_copy(it, i).start)
            pl.when(i % SUBS == SUBS - 1)(give_copy(it, i // SUBS, core).start)

    line_done = [0] * ITERS

    def run_both(stop):
        stop = min(stop, blocks + last_lag)
        start = line_done[0]
        if stop > start:
            def body(j, carry):
                line_step(0, start + j)
                line_step(1, begun + j)
                return carry

            begun = line_done[1]
            lax.fori_loop(0, stop - start, body, 0)
            line_done[0], line_done[1] = stop, begun + stop - start

    def run_line(it, stop):
        stop = min(stop, blocks + last_lag)
        if stop > line_done[it]:
            def body(j, carry):
                line_step(it, j)
                return carry

            lax.fori_loop(line_done[it], stop, body, 0)
            line_done[it] = stop

    def products(it, which):
        for g in which:
            span = group_rows(g)
            low = f_at[it][span, :].astype(jnp.bfloat16)
            f_low[span, :] = low
            product = jnp.dot(low, x_low[...], preferred_element_type=jnp.float32)
            misfit[span, :] = jnp.where(
                mask[span, :] != 0,
                product - obs[span, :].astype(jnp.float32),
                jnp.zeros_like(product),
            ).astype(jnp.bfloat16)

    def products_part(which, c):
        for g in which:
            span = group_rows(g)
            if c == 0:
                f_low[span, :] = f_in[span, :].astype(jnp.bfloat16)
            product = jnp.dot(f_low[span, :], x_low[:, columns(c)], preferred_element_type=jnp.float32)
            misfit[span, columns(c)] = jnp.where(
                mask[span, columns(c)] != 0,
                product - obs[span, columns(c)].astype(jnp.float32),
                jnp.zeros_like(product),
            ).astype(jnp.bfloat16)

    def series_grads(it, which):
        for g in which:
            span = group_rows(g)
            grad[it, span, :] = lax.dot_general(
                misfit[span, :], x_low[...], (((1,), (1,)), ((), ())), preferred_element_type=jnp.float32
            )

    def hour_grads(it, which):
        for g in which:
            span = group_rows(g)
            term = lax.dot_general(
                f_low[span, :], misfit[span, :], (((0,), (0,)), ((), ())), preferred_element_type=jnp.float32
            )
            if g > 0:
                term = g_loc[it] + term
            g_loc[it] = term

    def hour_grads_add(g, c):
        span = group_rows(g)
        g_loc[1, :, columns(c)] += lax.dot_general(
            f_low[span, :], misfit[span, columns(c)], (((0,), (0,)), ((), ())), preferred_element_type=jnp.float32
        )

    def hour_grads_part(it, c):
        g_loc[it, :, columns(c)] = lax.dot_general(
            f_low[...], misfit[:, columns(c)], (((0,), (0,)), ((), ())), preferred_element_type=jnp.float32
        )

    def start_pairs(it, which):
        for g in which:
            pair_copy(it, g).start()

    def start_up(it, c):
        for p in (0, series_size - 1):
            up_copy(it, p, c).start()

    def up_copy(it, p, c):
        forward = p < half
        to = p + 1 if forward else p - 1
        dst = up_in.at[it, to, :, columns(c)]
        return remote(
            g_loc.at[it, piece_rows(p), columns(c)], dst, up_send, up_recv.at[to - 1, c],
            following if forward else previous, tm,
        )

    def cross_copy(it, p, c):
        forward = p < half
        side = 1 if forward else 0
        return remote(
            g_loc.at[it, piece_rows(p), columns(c)], cross_in.at[it, side, :, columns(c)],
            cross_send, cross_recv.at[side, c], following if forward else previous, tm,
        )

    def share_slot(p):
        return p if p < half else p - 2

    def share_copy(it, p, c):
        forward = p < half
        to = p - 1 if forward else p + 1
        view = x_at[it + 1].at[piece_rows(p), columns(c)]
        return remote(
            view, view, share_send, share_recv.at[share_slot(to), c], previous if forward else following, tm,
        )

    def up_wait(it, p, c):
        slot = up_in.at[it, p, :, columns(c)]
        remote(slot, slot, up_send, up_recv.at[p - 1, c], following, tm).wait_recv()

    def cross_wait(it, side, c):
        slot = cross_in.at[it, side, :, columns(c)]
        remote(slot, slot, cross_send, cross_recv.at[side, c], following, tm).wait_recv()

    def share_wait(it, p, c):
        view = x_at[it + 1].at[piece_rows(p), columns(c)]
        remote(view, view, share_send, share_recv.at[share_slot(p), c], following, tm).wait_recv()

    def collect(it, depth, c):
        for p in (depth, series_size - 1 - depth):
            up_wait(it, p, c)
            total = g_loc[it, piece_rows(p), columns(c)] + up_in[it, p, :, columns(c)]
            if p == half - 1:
                total = total + lam_ar * ar[:, columns(c)]
            g_loc[it, piece_rows(p), columns(c)] = total
            (cross_copy if depth == half - 1 else up_copy)(it, p, c).start()

    def update(it, c):
        for p in (half - 1, half):
            side = p // half
            cross_wait(it, side, c)
            total = g_loc[it, piece_rows(p), columns(c)] + cross_in[it, side, :, columns(c)]
            old = x_at[it][piece_rows(p), columns(c)]
            x_at[it + 1][piece_rows(p), columns(c)] = old - step_x * (total + ridge_x * old)
            share_copy(it, p, c).start()

    def share(it, depth, c):
        for p in (depth, series_size - 1 - depth):
            share_wait(it, p, c)
            if depth > 0:
                share_copy(it, p, c).start()

    def residuals(it):
        x_now = x_at[it]
        to_right, to_left = edge_copies(it, x_now)

        @pl.when(tm > 0)
        def _():
            to_right.wait_recv()

        @pl.when(tm == 0)
        def _():
            halo_l[it] = jnp.zeros_like(halo_l[it])

        @pl.when(tm < tm_size - 1)
        def _():
            to_left.wait_recv()

        @pl.when(tm == tm_size - 1)
        def _():
            halo_r[it] = jnp.zeros_like(halo_r[it])

        extended = jnp.concatenate([halo_l[it], x_now[ar_rows, :], halo_r[it]], axis=1)
        width = hours + 2 * HALO
        weights = [w_cols[lag_at, ar_rows, :][:, 0:1] for lag_at in range(3)]
        resid = extended
        for lag_at in range(3):
            resid = resid - weights[lag_at] * pltpu.roll(extended, LAGS[lag_at], 1)
        hour = lax.broadcasted_iota(jnp.int32, (piece, width), 1) + (tm * hours - HALO)
        resid = jnp.where(both(hour >= 168, hour < hours_all), resid, jnp.zeros_like(resid))
        back = None
        for lag_at in range(3):
            term = weights[lag_at] * pltpu.roll(resid, width - LAGS[lag_at], 1)
            back = term if back is None else back + term
        ar[...] = (resid - back)[:, HALO : HALO + hours]

    ns = jax.named_scope

    def x_events(it):
        events = []
        for depth in range(1, half):
            events += [(collect, depth, c) for c in range(parts)]
        events += [(lambda it, _, c: update(it, c), 0, c) for c in range(parts)]
        for depth in range(half - 2, -1, -1):
            events += [(share, depth, c) for c in range(parts)]
        for e, (step, depth, c) in enumerate(events):
            with ns(f"zx{it}_{e}"):
                run_line(it, Z_AT_X[it] + Z_PER_X * e)
            with ns(f"x{it}_{e}"):
                step(it, depth, c)
            if it > 0 and e == 0:
                pl.when(not_end)(lambda: merge(1, last))

    every = tuple(range(groups))
    body_groups, next_last, last = every[1:-2], every[-2], every[-1]

    with ns("xload"):
        x_load.wait()
    x_low[...] = x_in[...].astype(jnp.bfloat16)
    with ns("load0"):
        for load_copy in first_loads:
            load_copy.wait()
    with ns("p0_0"):
        products(0, every[:1])
        series_grads(0, every[:1])
    with ns("barrier"):
        neighbours = jnp.minimum(tm, 2) + jnp.minimum(tm_size - 1 - tm, 2)
        pl.semaphore_wait(barrier, 2 + neighbours)
    start_pairs(0, every[:1])
    start_edges(0, x_in)
    start_outward_edges(0, x_in)
    with ns("load1"):
        f_load.wait()
    for c in range(parts):
        with ns(f"load2_{c}"):
            for load_copy in part_loads(c):
                load_copy.wait()
        with ns(f"p0_{c + 1}"):
            products_part(every[1:], c)
        if c == parts - 1:
            with ns("f0_1"):
                series_grads(0, every[1:2])
            start_pairs(0, every[1:2])
        with ns(f"g0_{c}"):
            hour_grads_part(0, c)
        start_up(0, c)
        if c == 0:
            with ns("m0_0"):
                merge(0, 0)
    with ns("f0_r"):
        series_grads(0, every[2:])
    start_pairs(0, every[2:])
    with ns("m0_1"):
        merge(0, 1)
    with ns("ar0"):
        w_load.wait()
        for lag_at in range(3):
            w_cols[lag_at] = jnp.transpose(jnp.broadcast_to(w_in[lag_at : lag_at + 1, :], (128, rank)))
        residuals(0)
    with ns("z0_a"):
        run_line(0, Z_FIRST)
    with ns("m0_r"):
        for g in every[2:]:
            merge(0, g)
    x_events(0)
    start_edges(1, x_mid)

    x_low[...] = x_mid[...].astype(jnp.bfloat16)
    def take(g):
        run_line(0, (g + 1) * SUBS + last_lag)
        give_copy(0, g, 1 - core).wait_recv()

    for g in every[:-2]:
        with ns(f"t1_{g}"):
            take(g)
        with ns(f"p1_{g}"):
            products(1, (g,))
            series_grads(1, (g,))
        start_pairs(1, (g,))
        with ns(f"zm1_{g}"):
            run_line(0, Z_MID[min(g, len(Z_MID) - 1)])
        if g > 0:
            with ns(f"m1_{g - 1}"):
                merge(1, g - 1)
    with ns("g1_a"):
        hour_grads(1, every[:-2])
    with ns("t1_c"):
        run_line(0, Z_MID[-1])
        take(next_last)
    start_outward_edges(1, x_mid)
    with ns("z1_1"):
        run_line(1, Z_NEXT)
    with ns("p1_c"):
        products(1, (next_last,))
        series_grads(1, (next_last,))
        hour_grads(1, (next_last,))
    start_pairs(1, (next_last,))
    with ns("m1_b"):
        merge(1, next_last - 1)
    with ns("t1_d"):
        run_both((last + 1) * SUBS + last_lag)
        take(last)
    with ns("p1_d"):
        products(1, (last,))
        hour_grads_add(last, 0)
    start_up(1, 0)
    with ns("p1_e"):
        for c in range(1, parts):
            hour_grads_add(last, c)
    for c in range(1, parts):
        start_up(1, c)
    with ns("z1_a"):
        run_line(1, Z_LAST[0])
    with ns("f1_d"):
        series_grads(1, (last,))
    start_pairs(1, (last,))
    with ns("m1_c"):
        merge(1, next_last)
    with ns("z1_b"):
        run_line(1, Z_LAST[1])
    with ns("ar1"):
        residuals(1)
    with ns("z1_c"):
        run_line(1, Z_LAST[2])
    with ns("m1_d"):
        pl.when(is_end)(lambda: merge(1, last))
    x_events(1)
    with ns("zend"):
        run_line(1, blocks + last_lag)
    with ns("gend"):
        for g in every:
            give_copy(1, g, 1 - core).wait_recv()
    sc = ns("drain"); sc.__enter__()

    def sent(view, sem):
        remote(view, view, sem, cross_recv.at[0, 0], following, tm).wait_send()

    pl.when(tm < tm_size - 1)(lambda: sent(halo_l, right_send))
    pl.when(tm > 0)(lambda: sent(halo_r, left_send))
    for sem in (pair_send, in_send, give_send):
        sent(grad.at[0], sem)
    pl.when(not_end)(lambda: sent(grad.at[0], spread_send))
    many = up_in.at[:, pl.ds(0, series_size - 2)]
    sent(many, up_send)
    sent(many, share_send)
    sent(cross_in, cross_send)
    sc.__exit__(None, None, None)


def final_product(f_ref, x_ref, f_out, x_out, imputed, x_low, low, copy_sem, out_sem):
    rows = f_ref.shape[0]
    copies = [
        pltpu.make_async_copy(f_ref, f_out, copy_sem.at[0]),
        pltpu.make_async_copy(x_ref, x_out, copy_sem.at[1]),
    ]
    for c in copies:
        c.start()
    x_low[...] = x_ref[...].astype(jnp.bfloat16)
    for i in range(pl.cdiv(rows, TALL)):
        span = pl.ds(i * TALL, min(TALL, rows - i * TALL))
        low[span, :] = jnp.dot(
            f_ref[span, :].astype(jnp.bfloat16), x_low[...], preferred_element_type=jnp.float32
        ).astype(jnp.bfloat16)
        copies.append(pltpu.make_async_copy(low.at[span, :], imputed.at[span, :], out_sem.at[i]))
        copies[-1].start()
    for c in copies:
        c.wait()


def solution(mesh):
    series_size, tm_size = mesh.shape["series"], mesh.shape["tm"]

    def local(observed, mask, series_factors, time_factors, ar_weights):
        rows, rank = series_factors.shape
        hours = time_factors.shape[1]
        groups = rows // GROUP
        blocks = groups * SUBS
        parts = hours // WIDTH
        piece = rank // series_size
        f32, bf16 = jnp.float32, jnp.bfloat16
        vmem = pl.BlockSpec(memory_space=pltpu.VMEM)
        hbm = pl.BlockSpec(memory_space=pltpu.HBM)
        dma = pltpu.SemaphoreType.DMA
        line = (ITERS, rows // 2, rank)
        f_last, x_last = pl.pallas_call(
            functools.partial(kernel, series_size, tm_size),
            out_shape=(pltpu.VMEM((rows, rank), f32), pltpu.VMEM((rank, hours), f32)),
            in_specs=[hbm] * 5,
            out_specs=(vmem, vmem),
            scratch_shapes=[
                pltpu.VMEM((rows, hours), bf16),
                pltpu.VMEM((rows, hours), jnp.int32),
                pltpu.VMEM((rows, rank), f32),
                pltpu.VMEM((rank, hours), f32),
                pltpu.VMEM((rows, rank), f32),
                pltpu.VMEM((rank, hours), f32),
                pltpu.VMEM((piece, hours), f32),
                pltpu.VMEM((rows, hours), bf16),
                pltpu.VMEM((rows, rank), bf16),
                pltpu.VMEM((rank, hours), bf16),
                pltpu.VMEM((ITERS, rows, rank), f32),
                pltpu.VMEM(line, f32),
                pltpu.VMEM(line, f32),
                pltpu.VMEM(line, f32),
                pltpu.VMEM((ITERS, rank, hours), f32),
                pltpu.VMEM((ITERS, series_size, piece, hours), f32),
                pltpu.VMEM((ITERS, 2, piece, hours), f32),
                pltpu.VMEM((ITERS, piece, HALO), f32),
                pltpu.VMEM((ITERS, piece, HALO), f32),
                pltpu.VMEM((3, rank), f32),
                pltpu.VMEM((3, rank, 128), f32),
                dma((6 + 2 * parts,)),
                dma((groups,)), dma((groups,)),
                dma((blocks,)), dma((blocks + LAG + 1,)),
                dma((series_size - 2, parts)), dma((2, parts)), dma((series_size - 2, parts)),
                dma((ITERS, 2)),
            ],
            compiler_params=pltpu.CompilerParams(
                collective_id=0, has_side_effects=True,
                vmem_limit_bytes=VMEM_BYTES - 4 * rank * (rows + hours) - VMEM_SPARE,
            ),
        )(observed, mask, series_factors, time_factors, ar_weights)
        anywhere = pl.BlockSpec(memory_space=pl.ANY)
        return tuple(pl.pallas_call(
            final_product,
            out_shape=(
                jax.ShapeDtypeStruct((rows, rank), f32),
                jax.ShapeDtypeStruct((rank, hours), f32),
                jax.ShapeDtypeStruct((rows, hours), bf16),
            ),
            in_specs=[vmem, vmem],
            out_specs=(anywhere, anywhere, anywhere),
            scratch_shapes=[
                pltpu.VMEM((rank, hours), bf16),
                pltpu.VMEM((rows, hours), bf16),
                dma((2,)),
                dma((pl.cdiv(rows, TALL),)),
            ],
            compiler_params=pltpu.CompilerParams(vmem_limit_bytes=16 * 1024 * 1024),
        )(f_last, x_last))

    in_specs = (P("series", "tm"), P("series", "tm"), P("series", None), P(None, "tm"), P())
    out_specs = (P("series", None), P(None, "tm"), P("series", "tm"))
    return jax.shard_map(local, mesh=mesh, in_specs=in_specs, out_specs=out_specs, check_vma=False)
```
